32 devices in a mesh: seq: 8 (over y, x, core), head: 4 (over z).
Axes of the slice: x: 2, y: 2, z: 4, core: 2. Of those that a mesh axis runs over, the one named last changes fastest.
Arguments:
- queries: bfloat16 [3, 2048, 2048], P(None, 'seq', 'head'), may hold values from -24 to 24
- key_vectors: bfloat16 [4, 2048, 2048], P(None, 'seq', 'head'), may hold values from -24 to 24
- values: bfloat16 [4, 2048, 2048], P(None, 'seq', 'head'), may hold values from -6 to 6
- learn_rates: float32 [3, 2048, 4], P(None, 'seq', 'head'), may hold values from 0.001 to 0.01
- norm_gain: float32 [2048], P('head'), may hold values from 0.1 to 1.9
- out_weight: bfloat16 [2048, 2048], P('head'), may hold values from -0.125 to 0.125
- incoming: float32 [8, 4, 3, 512, 512], P('seq', 'head'), may hold values from -0.25 to 0.25
Outputs:
- mixed_out: bfloat16 [3, 2048, 2048], P(None, 'seq', 'head')
- outgoing: float32 [8, 4, 3, 512, 512], P('seq', 'head')
The draws below stay inside these ranges and needn't reach their ends.
All inputs are finite; a program needn't handle non-finite values.
Results may differ from the reference program's by a relative error of at most 0.013.
The reference program's roundings to bfloat16 on the way count: a program that leaves them out, or rounds other values in their place, can miss the bound.
Values may be sent and summed in bfloat16 or wider, within the bound.
A program may use at most 64 MiB of HBM per device.

```python
import math
import jax
import jax.numpy as jnp
from jax import lax

HEADS = 4
HD = 512
GROUP = 256
TICKS = 3
WIDTH = 2048
SEQ_TOK = 2048
N_SEQ = 8


def paired_draw(key):
    key_raw = jax.random.normal(jax.random.fold_in(key, 101), (TICKS + 1, SEQ_TOK, WIDTH), jnp.float32)
    query_raw = jax.random.normal(jax.random.fold_in(key, 202), (TICKS, SEQ_TOK, WIDTH), jnp.float32)
    return (jnp.clip(key_raw, -24.0, 24.0), jnp.clip(query_raw, -24.0, 24.0))


def draw_queries(key, part):
    return paired_draw(key)[1].astype(jnp.bfloat16)


def draw_key_vectors(key, part):
    return paired_draw(key)[0].astype(jnp.bfloat16)


def levels(rng, shape, cuts, low, largest):
    def one(axis_at, shards_of):
        draws = jax.random.uniform(jax.random.fold_in(jax.random.fold_in(rng, 6), axis_at), (shards_of,), jnp.float32, low / len(cuts), largest / len(cuts))
        return jnp.repeat(jnp.exp(draws), shape[axis_at] // shards_of).reshape((-1,) + (1,) * (len(shape) - axis_at - 1))

    gain = one(*cuts[0])
    for cut in cuts[1:]:
        gain = gain * one(*cut)
    return gain


def centred(rng, dims, deviation, reach, shards=(), dtype=jnp.bfloat16):
    factor_of = levels(rng, dims, shards, -0.22, 0.18) if shards else 1.0
    entries = jax.random.normal(rng, dims, jnp.float32) * deviation * factor_of
    return jnp.minimum(jnp.maximum(entries, -reach), reach).astype(dtype)


def setup_inputs(seed: int = 0) -> dict:
    key_list = jax.random.split(jax.random.key(seed), 8)
    return {
        "queries": draw_queries(jax.random.fold_in(key_list[7], 71), 0),
        "key_vectors": draw_key_vectors(jax.random.fold_in(key_list[7], 71), 0),
        "values": centred(key_list[2], (TICKS + 1, SEQ_TOK, WIDTH), 1.0, 6.0, ((1, 8), (2, 4))),
        "learn_rates": jnp.clip(jnp.exp(math.log(0.01) - 2.30258502 * jax.random.uniform(key_list[3], (TICKS, SEQ_TOK, HEADS), jnp.float32) ** levels(key_list[3], (TICKS, SEQ_TOK, HEADS), ((1, 8), (2, 4)), -0.2, 0.2)), 0.001, 0.01),
        "norm_gain": jnp.clip(1.0 + 0.18 * jax.random.normal(key_list[4], (WIDTH,), jnp.float32), 0.1, 1.9),
        "out_weight": centred(key_list[5], (WIDTH, WIDTH), WIDTH ** -0.5, 0.125, ((0, 4),)),
        "incoming": centred(key_list[6], (N_SEQ, HEADS, 3, HD, HD), HD ** -0.5, 0.25, ((0, 8), (1, 4)), jnp.float32),
    }


def fast_apply(rounded, query_rows):
    first_proj = jnp.dot(query_rows, rounded[0], preferred_element_type=jnp.float32)
    third_proj = jnp.dot(query_rows, rounded[1], preferred_element_type=jnp.float32)
    hidden = (first_proj * jax.nn.sigmoid(first_proj) * third_proj).astype(jnp.bfloat16)
    return jnp.dot(hidden, rounded[2], preferred_element_type=jnp.float32)

def fast_update(fast_state, rounded, key_rows, scaled_values):
    first_proj = jnp.dot(key_rows, rounded[0], preferred_element_type=jnp.float32)
    third_proj = jnp.dot(key_rows, rounded[1], preferred_element_type=jnp.float32)
    gate_sig = jax.nn.sigmoid(first_proj)
    hidden = (first_proj * gate_sig * third_proj).astype(jnp.bfloat16)
    grad_down = jnp.dot(hidden.T, scaled_values, preferred_element_type=jnp.float32)
    back_grad = jnp.dot(scaled_values, rounded[2].T, preferred_element_type=jnp.float32)
    grad_first = (back_grad * third_proj * gate_sig * (1.0 + first_proj * (1.0 - gate_sig))).astype(jnp.bfloat16)
    grad_third = (back_grad * first_proj * gate_sig).astype(jnp.bfloat16)
    grad_one = jnp.dot(key_rows.T, grad_first, preferred_element_type=jnp.float32)
    grad_three = jnp.dot(key_rows.T, grad_third, preferred_element_type=jnp.float32)
    stepped = fast_state + jnp.stack([grad_one, grad_three, grad_down])
    before_sq = lax.optimization_barrier(jnp.mean(fast_state * fast_state, axis=1, keepdims=True))
    after_sq = lax.optimization_barrier(jnp.mean(stepped * stepped, axis=1, keepdims=True))
    return stepped * jnp.sqrt((before_sq + 1e-06) / (after_sq + 1e-06))

def window_attend(query_rows, prior_keys, own_keys, prior_vals, own_vals):
    length = query_rows.shape[0]
    joined_keys = jnp.concatenate([prior_keys, own_keys], axis=0)
    joined_vals = jnp.concatenate([prior_vals, own_vals], axis=0)
    scores = jnp.dot(query_rows, joined_keys.T, preferred_element_type=jnp.float32) * query_rows.shape[1] ** (-0.5)
    query_pos = jnp.arange(length)[:, None] + length
    key_pos = jnp.arange(2 * length)[None, :]
    allowed = (key_pos <= query_pos) & (key_pos > query_pos - length)
    scores = jnp.where(allowed, scores, -1e+30)
    peak = lax.optimization_barrier(jnp.max(scores, axis=1, keepdims=True))
    expo = jnp.exp(scores - peak)
    probs = (expo / lax.optimization_barrier(jnp.sum(expo, axis=1, keepdims=True))).astype(jnp.bfloat16)
    return jnp.dot(probs, joined_vals, preferred_element_type=jnp.float32)

def mix_head(fast_out, attended, gain_row):
    normed = fast_out * lax.rsqrt(lax.optimization_barrier(jnp.mean(fast_out * fast_out, axis=1, keepdims=True)) + 1e-06) * gain_row
    return (attended + normed).astype(jnp.bfloat16)

def one_head(fast_state, query_rows, prior_keys, own_keys, prior_vals, own_vals, rate_rows, gain_row):
    rounded = fast_state.astype(jnp.bfloat16)
    fast_out = fast_apply(rounded, query_rows)
    scaled_values = (rate_rows[:, None] * own_vals.astype(jnp.float32)).astype(jnp.bfloat16)
    updated = fast_update(fast_state, rounded, own_keys, scaled_values)
    attended = window_attend(query_rows, prior_keys, own_keys, prior_vals, own_vals)
    return (mix_head(fast_out, attended, gain_row), updated)

def reference(queries, key_vectors, values, learn_rates, norm_gain, out_weight, incoming):
    query_all = queries.reshape(TICKS, N_SEQ, GROUP, HEADS, HD)
    key_all = key_vectors.reshape(TICKS + 1, N_SEQ, GROUP, HEADS, HD)
    value_all = values.reshape(TICKS + 1, N_SEQ, GROUP, HEADS, HD)
    rate_all = learn_rates.reshape(TICKS, N_SEQ, GROUP, HEADS)
    gains = norm_gain.reshape(HEADS, HD)
    rows_out = out_weight.reshape(HEADS, HD, WIDTH)
    per_head = jax.vmap(one_head, in_axes=(0, 1, 1, 1, 1, 1, 1, 0))

    def one_block(inputs):
        fast_state, query_rows, prior_keys, own_keys, prior_vals, own_vals, rate_rows = inputs
        combined, updated = per_head(fast_state, query_rows, prior_keys, own_keys, prior_vals, own_vals, rate_rows, gains)
        total = jnp.zeros((GROUP, WIDTH), jnp.float32)
        for head_index in range(HEADS):
            partial_value = jnp.dot(combined[head_index], rows_out[head_index], preferred_element_type=jnp.float32).astype(jnp.bfloat16)
            partial_value = lax.optimization_barrier(partial_value)
            total = total + partial_value.astype(jnp.float32)
        return (total.astype(jnp.bfloat16), updated)
    fast_states = incoming
    outputs = []
    for tick_index in range(TICKS):
        mixed, updated = lax.map(one_block, (fast_states, query_all[tick_index], jnp.roll(key_all[tick_index], 1, axis=0), key_all[tick_index + 1], jnp.roll(value_all[tick_index], 1, axis=0), value_all[tick_index + 1], rate_all[tick_index]))
        outputs.append(mixed.reshape(SEQ_TOK, WIDTH))
        if tick_index + 1 < TICKS:
            fast_states = jnp.roll(updated, 1, axis=0)
        else:
            fast_states = updated
    return (jnp.stack(outputs), fast_states)
```

```python
import functools

import jax
import jax.numpy as jnp
from jax import lax
from jax.experimental import pallas as pl
from jax.experimental.pallas import tpu as pltpu
from jax.sharding import PartitionSpec as P


F32, BF16 = jnp.float32, jnp.bfloat16
MESH = pl.DeviceIdType.MESH
WEIGHTS = (0, 1, 2)
LATE_PIECES = 2


def dot(a, b, over=(1, 0)):
    return lax.dot_general(a, b, (((over[0],), (over[1],)), ((), ())), preferred_element_type=F32)


def normed_apply(rounded, query_rows, gain_row):
    first_proj = dot(query_rows, rounded[0]())
    third_proj = dot(query_rows, rounded[1]())
    hidden = (first_proj * jax.nn.sigmoid(first_proj) * third_proj).astype(BF16)
    fast_out = dot(hidden, rounded[2]())
    mean_sq = jnp.mean(fast_out * fast_out, axis=1, keepdims=True)
    return fast_out * lax.rsqrt(mean_sq + 1e-06) * gain_row


def fast_update(olds, rounded, key_rows, scaled_values, put_new):
    first_proj = dot(key_rows, rounded[0]())
    third_proj = dot(key_rows, rounded[1]())
    gate_sig = jax.nn.sigmoid(first_proj)
    gated = first_proj * gate_sig

    def put(i, grad):
        old = olds[i]()
        stepped = old + grad
        before_sq = jnp.mean(old * old, axis=0, keepdims=True)
        after_sq = jnp.mean(stepped * stepped, axis=0, keepdims=True)
        put_new(i, stepped * jnp.sqrt((before_sq + 1e-06) / (after_sq + 1e-06)))

    back_grad = dot(scaled_values, rounded[2](), (1, 1))
    slope = gate_sig * (1.0 + first_proj * (1.0 - gate_sig))
    put(0, dot(key_rows, (back_grad * third_proj * slope).astype(BF16), (0, 0)))
    put(1, dot(key_rows, (back_grad * gated).astype(BF16), (0, 0)))
    hidden = (gated * third_proj).astype(BF16)
    put(2, dot(hidden, scaled_values, (0, 0)))


def softmax_parts(scores, own):
    expo = jnp.exp(scores - jnp.max(scores, axis=1, keepdims=True))
    probs = expo / jnp.sum(expo, axis=1, keepdims=True)
    zero = jnp.zeros_like(probs)
    return jnp.where(own, probs, zero).astype(BF16), jnp.where(own, zero, probs).astype(BF16)


def attend_rows(query_rows, prior, own, low, high):
    size = query_rows.shape[1]
    length = own.length
    scale = size ** (-0.5)
    span = high - low
    pieces = []
    if low:
        pieces.append(dot(query_rows, own.keys(0, low), (1, 1)))
    row = lax.broadcasted_iota(jnp.int32, (span, span), 0)
    col = lax.broadcasted_iota(jnp.int32, (span, span), 1)
    pieces.append(
        jnp.where(
            col <= row,
            dot(query_rows, own.keys(low, high), (1, 1)),
            dot(query_rows, prior.keys(low, high), (1, 1)),
        )
    )
    if high < length:
        pieces.append(dot(query_rows, prior.keys(high, length), (1, 1)))
    scores = (jnp.concatenate(pieces, axis=1) if len(pieces) > 1 else pieces[0]) * scale
    row = lax.broadcasted_iota(jnp.int32, (span, length), 0) + low
    is_own = lax.broadcasted_iota(jnp.int32, (span, length), 1) <= row
    own_probs, prior_probs = softmax_parts(scores, is_own)
    return dot(own_probs[:, :high], own.values(0, high)) + dot(
        prior_probs[:, low:], prior.values(low, length)
    )


class Rows:
    def __init__(self, keys_ref, values_ref):
        self.k, self.v, self.length = keys_ref, values_ref, keys_ref.shape[0]

    def keys(self, a, b):
        return self.k[a:b]

    def values(self, a, b):
        return self.v[a:b]


def layer_kernel(
    q_hbm, k_hbm, v_hbm, rate_hbm, gain_hbm, ow_hbm, w_hbm,
    out_ref, new_ref,
    q, k, v, rate, gain, ow, w,
    near, w_send, w_recv, z_send, z_recv, z_keep, z_fwd, z_last, z_own,
    in_sem, near_s, near_r, w_s, w_r, z1_s, z1_r, z2_s, z2_r,
):
    ticks, rows, size = q.shape
    last = ticks - 1
    n_seq, n_head = lax.axis_size("seq"), lax.axis_size("head")
    s, h = lax.axis_index("seq"), lax.axis_index("head")
    nxt, prv = lax.rem(s + 1, n_seq), lax.rem(s + n_seq - 1, n_seq)
    odd = lax.rem(s, 2)
    side = h + 1 - 2 * lax.rem(h, 2)
    mirror = n_head - 1 - h
    across = lax.rem(h + n_head // 2, n_head)
    first = side + odd * (mirror - side)
    second = mirror + odd * (side - mirror)

    loads = []

    def load(src, dst):
        copy = pltpu.make_async_copy(src, dst, in_sem.at[len(loads)])
        copy.start()
        loads.append(copy)
        return copy

    get_k = [None] * ticks
    get_v = [None] * ticks
    get_q = [None] * ticks
    get_k[0] = load(k_hbm.at[1], k.at[0])
    get_w = [load(w_hbm.at[0, 0, i], w.at[i]) for i in WEIGHTS]
    get_v[0] = load(v_hbm.at[1], v.at[0])
    get_rate = load(rate_hbm, rate)

    barrier = pltpu.get_barrier_semaphore()
    for who in ({"seq": nxt}, {"seq": prv}, {"head": side}, {"head": mirror}):
        pl.semaphore_signal(barrier, inc=1, device_id=who, device_id_type=MESH)

    get_q[0] = load(q_hbm.at[0], q.at[0])
    get_gain = load(gain_hbm, gain)
    get_ow = load(ow_hbm, ow)
    for t in range(1, ticks):
        get_k[t] = load(k_hbm.at[t + 1], k.at[t])
        get_v[t] = load(v_hbm.at[t + 1], v.at[t])
        get_q[t] = load(q_hbm.at[t], q.at[t])
    pl.semaphore_wait(barrier, 4)

    sent = []

    def remote(src, dst, ss, rs, who):
        return pltpu.make_async_remote_copy(
            src_ref=src, dst_ref=dst, send_sem=ss, recv_sem=rs, device_id=who, device_id_type=MESH
        )

    def push(copy):
        copy.start()
        sent.append(copy)

    step = rows // LATE_PIECES

    def near_copies(t):
        cuts = [(0, rows)] if t < last else [(i * step, (i + 1) * step) for i in reversed(range(LATE_PIECES))]
        found = []
        for j, (a, b) in enumerate(cuts):
            for i, hbm in enumerate((k_hbm, v_hbm)):
                at = (t, j, i)
                found.append(
                    remote(
                        hbm.at[t, pl.ds(a, b - a)], near.at[t, i, pl.ds(a, b - a)],
                        near_s.at[at], near_r.at[at], {"seq": nxt},
                    )
                )
        return found

    def send_near(t):
        for copy in near_copies(t):
            push(copy)

    def w_copy(t, i):
        return remote(w_send.at[t, i], w_recv.at[t, i], w_s.at[t, i], w_r.at[t, i], {"seq": nxt})

    def sv_of(t):
        column = jnp.broadcast_to(rate[t : t + 1], (8, rows)).T[:, :1]
        return (column * v[t].astype(F32)).astype(BF16)

    def z_first(t, a, b, j, i):
        return remote(
            z_send.at[t, i, pl.ds(a, b - a)], z_recv.at[t, i, pl.ds(a, b - a)],
            z1_s.at[t, j, i], z1_r.at[t, j, i], {"head": first},
        )

    def z_second(t, a, b, j):
        return remote(
            z_fwd.at[t, pl.ds(a, b - a)], z_last.at[t, pl.ds(a, b - a)],
            z2_s.at[t, j], z2_r.at[t, j], {"head": second},
        )

    def project(combined, t, a, b, j):
        def piece(target):
            columns = pl.ds(pl.multiple_of(target * size, 128), size)
            return dot(combined, ow[:, columns]).astype(BF16)

        for i, target in enumerate((across, first)):
            z_send[t, i, a:b] = piece(target)
            push(z_first(t, a, b, j, i))
        z_keep[t, 0, a:b] = piece(second)
        z_keep[t, 1, a:b] = piece(h)

    def pass_on(t, a, b, j):
        z_first(t, a, b, j, 0).wait_recv()
        z_fwd[t, a:b] = (z_keep[t, 0, a:b].astype(F32) + z_recv[t, 0, a:b].astype(F32)).astype(BF16)
        push(z_second(t, a, b, j))
        z_first(t, a, b, j, 1).wait_recv()
        z_own[t, a:b] = z_keep[t, 1, a:b].astype(F32) + z_recv[t, 1, a:b].astype(F32)

    def finish(t, a, b, j):
        z_second(t, a, b, j).wait_recv()
        out_ref[t, a:b] = (z_own[t, a:b] + z_last[t, a:b].astype(F32)).astype(BF16)

    def waiting(copy, read):
        done = []

        def get():
            if not done:
                copy.wait()
                done.append(True)
            return read()

        return get

    def arrived(t, i):
        done = []

        def get():
            if not done:
                w_copy(t, i).wait_recv()
                done.append(True)
            return w_recv[t, i]

        return get

    own = [Rows(k.at[t], v.at[t]) for t in range(ticks)]
    prior = [Rows(near.at[t, 0], near.at[t, 1]) for t in range(ticks)]
    state = [waiting(get_w[i], lambda i=i: w[i]) for i in WEIGHTS]
    rounded = [lambda i=i: state[i]().astype(BF16) for i in WEIGHTS]
    send_near(0)

    for t in range(ticks):
        get_k[t].wait()
        get_v[t].wait()
        if t == 0:
            get_rate.wait()

        def update():
            def store(i, x):
                if t < last:
                    w_send[t, i] = x.astype(BF16)
                    push(w_copy(t, i))
                else:
                    new_ref[0, 0, i] = x

            fast_update(state, rounded, k[t], sv_of(t), store)
            if t < last:
                send_near(t + 1)

        def apply():
            get_q[t].wait()
            if t == 0:
                get_gain.wait()
            return normed_apply(rounded, q[t], gain[...])

        if t < last:
            update()
            normed = apply()
        else:
            normed = apply()
            update()
        if t == 0:
            get_ow.wait()
        if t < last:
            for copy in near_copies(t):
                copy.wait_recv()
            att = attend_rows(q[t], prior[t], own[t], 0, rows)
            project((att + normed).astype(BF16), t, 0, rows, 0)
            if t:
                finish(t - 1, 0, rows, 0)
            pass_on(t, 0, rows, 0)
            rounded = [arrived(t, i) for i in WEIGHTS]
            state = [lambda f=f: f().astype(F32) for f in rounded]
        else:
            finish(t - 1, 0, rows, 0)
            cuts = [(i * step, (i + 1) * step) for i in reversed(range(LATE_PIECES))]
            copies = near_copies(t)
            for j, (a, b) in enumerate(cuts):
                for copy in copies[2 * j : 2 * j + 2]:
                    copy.wait_recv()
                att = attend_rows(q[t, a:b], prior[t], own[t], a, b)
                project((att + normed[a:b]).astype(BF16), t, a, b, j)
            for j, (a, b) in enumerate(cuts):
                pass_on(t, a, b, j)
            for j, (a, b) in enumerate(cuts):
                finish(t, a, b, j)
    for copy in sent:
        copy.wait_send()


def on_device(queries, key_vectors, values, learn_rates, norm_gain, out_weight, incoming):
    ticks, rows, size = queries.shape
    any_space = pl.BlockSpec(memory_space=pl.ANY)
    vmem = pl.BlockSpec(memory_space=pltpu.VMEM)
    dma = pltpu.SemaphoreType.DMA
    block = (ticks, rows, size)
    matrices = (len(WEIGHTS), size, size)
    scratch = [
        pltpu.VMEM(block, BF16),
        pltpu.VMEM(block, BF16),
        pltpu.VMEM(block, BF16),
        pltpu.VMEM((ticks, rows), F32),
        pltpu.VMEM((1, size), F32),
        pltpu.VMEM(out_weight.shape, BF16),
        pltpu.VMEM(matrices, F32),
        pltpu.VMEM((ticks, 2, rows, size), BF16),
        pltpu.VMEM((ticks - 1, *matrices), BF16),
        pltpu.VMEM((ticks - 1, *matrices), BF16),
        pltpu.VMEM((ticks, 2, rows, size), BF16),
        pltpu.VMEM((ticks, 2, rows, size), BF16),
        pltpu.VMEM((ticks, 2, rows, size), BF16),
        pltpu.VMEM(block, BF16),
        pltpu.VMEM(block, BF16),
        pltpu.VMEM(block, F32),
        dma((6 + 3 * ticks,)),
        dma((ticks, LATE_PIECES, 2)),
        dma((ticks, LATE_PIECES, 2)),
        dma((ticks - 1, len(WEIGHTS))),
        dma((ticks - 1, len(WEIGHTS))),
        dma((ticks, LATE_PIECES, 2)),
        dma((ticks, LATE_PIECES, 2)),
        dma((ticks, LATE_PIECES)),
        dma((ticks, LATE_PIECES)),
    ]
    out, outgoing = pl.pallas_call(
        layer_kernel,
        out_shape=[
            jax.ShapeDtypeStruct(queries.shape, BF16),
            jax.ShapeDtypeStruct(incoming.shape, F32),
        ],
        in_specs=[any_space] * 7,
        out_specs=[vmem, vmem],
        scratch_shapes=scratch,
        compiler_params=pltpu.CompilerParams(
            collective_id=0, has_side_effects=True, vmem_limit_bytes=60 << 20
        ),
        name="layer_kernel",
    )(
        queries, key_vectors, values, learn_rates.reshape(ticks, rows), norm_gain.reshape(1, size),
        out_weight, incoming,
    )
    return out, outgoing


def solution(mesh):
    placed = (
        P(None, "seq", "head"),
        P(None, "seq", "head"),
        P(None, "seq", "head"),
        P(None, "seq", "head"),
        P("head"),
        P("head", None),
        P("seq", "head", None, None, None),
    )
    return jax.shard_map(
        on_device,
        mesh=mesh,
        in_specs=placed,
        out_specs=(P(None, "seq", "head"), P("seq", "head", None, None, None)),
        check_vma=False,
    )
```

```python
import functools

import jax
import jax.numpy as jnp
from jax import lax
from jax.experimental import pallas as pl
from jax.experimental.pallas import tpu as pltpu
from jax.sharding import PartitionSpec as P


F32, BF16 = jnp.float32, jnp.bfloat16
MESH = pl.DeviceIdType.MESH
WEIGHTS = (0, 1, 2)
LATE_PIECES = 4
LANES = 128


def dot(a, b, over=(1, 0)):
    return lax.dot_general(a, b, (((over[0],), (over[1],)), ((), ())), preferred_element_type=F32)


def normed_apply(rounded, query_rows, gain_row):
    first_proj = dot(query_rows, rounded[0]())
    third_proj = dot(query_rows, rounded[1]())
    hidden = (first_proj * jax.nn.sigmoid(first_proj) * third_proj).astype(BF16)
    fast_out = dot(hidden, rounded[2]())
    mean_sq = jnp.mean(fast_out * fast_out, axis=1, keepdims=True)
    return fast_out * lax.rsqrt(mean_sq + 1e-06) * gain_row


def fast_update(olds, rounded, key_rows, scaled_values, put_new):
    first_proj = dot(key_rows, rounded[0]())
    third_proj = dot(key_rows, rounded[1]())
    gate_sig = jax.nn.sigmoid(first_proj)
    gated = first_proj * gate_sig

    def put(i, grad):
        old = olds[i]()
        stepped = old + grad
        before_sq = jnp.mean(old * old, axis=0, keepdims=True)
        after_sq = jnp.mean(stepped * stepped, axis=0, keepdims=True)
        put_new(i, stepped * jnp.sqrt((before_sq + 1e-06) / (after_sq + 1e-06)))

    back_grad = dot(scaled_values, rounded[2](), (1, 1))
    slope = gate_sig * (1.0 + first_proj * (1.0 - gate_sig))
    put(0, dot(key_rows, (back_grad * third_proj * slope).astype(BF16), (0, 0)))
    put(1, dot(key_rows, (back_grad * gated).astype(BF16), (0, 0)))
    hidden = (gated * third_proj).astype(BF16)
    put(2, dot(hidden, scaled_values, (0, 0)))


def softmax_parts(scores, own):
    expo = jnp.exp(scores - jnp.max(scores, axis=1, keepdims=True))
    probs = expo / jnp.sum(expo, axis=1, keepdims=True)
    zero = jnp.zeros_like(probs)
    return jnp.where(own, probs, zero).astype(BF16), jnp.where(own, zero, probs).astype(BF16)


def own_scores(query_rows, own):
    return dot(query_rows, own.keys(0, own.length), (1, 1))


def attend_rows(query_rows, scores_own, prior, own, low):
    span, size = query_rows.shape
    length = own.length
    reach = min(length, -(-(low + span) // LANES) * LANES)

    def joined(part_own, part_prior):
        if not low:
            return part_prior(0, length)
        return jnp.concatenate([part_own(0, low), part_prior(low, length)], axis=0)

    row = lax.broadcasted_iota(jnp.int32, (span, length), 0) + low
    is_own = lax.broadcasted_iota(jnp.int32, (span, length), 1) <= row
    other = dot(query_rows, joined(own.keys, prior.keys), (1, 1))
    scores = jnp.where(is_own, scores_own, other) * size ** (-0.5)
    own_probs, prior_probs = softmax_parts(scores, is_own)
    return dot(own_probs[:, :reach], own.values(0, reach)) + dot(
        prior_probs, joined(own.values, prior.values)
    )


class Rows:
    def __init__(self, keys_ref, values_ref):
        self.k, self.v, self.length = keys_ref, values_ref, keys_ref.shape[0]

    def keys(self, a, b):
        return self.k[a:b]

    def values(self, a, b):
        return self.v[a:b]


def layer_kernel(
    q_hbm, k_hbm, v_hbm, rate_hbm, gain_hbm, ow_hbm, w_hbm,
    out_ref, new_ref,
    q, k, v, rate, gain, ow, w,
    near, w_send, w_recv, z_send, z_recv, z_keep, z_fwd, z_last, z_own,
    in_sem, near_s, near_r, w_s, w_r, z1_s, z1_r, z2_s, z2_r,
):
    ticks, rows, size = q.shape
    last = ticks - 1
    n_seq, n_head = lax.axis_size("seq"), lax.axis_size("head")
    s, h = lax.axis_index("seq"), lax.axis_index("head")
    nxt, prv = lax.rem(s + 1, n_seq), lax.rem(s + n_seq - 1, n_seq)
    odd = lax.rem(s, 2)
    side = h + 1 - 2 * lax.rem(h, 2)
    mirror = n_head - 1 - h
    across = lax.rem(h + n_head // 2, n_head)
    first, second = side, mirror

    loads = []

    def load(src, dst):
        copy = pltpu.make_async_copy(src, dst, in_sem.at[len(loads)])
        copy.start()
        loads.append(copy)
        return copy

    get_k = [None] * ticks
    get_v = [None] * ticks
    get_q = [None] * ticks
    get_k[0] = load(k_hbm.at[1], k.at[0])
    get_w = [load(w_hbm.at[0, 0, i], w.at[i]) for i in WEIGHTS]
    get_v[0] = load(v_hbm.at[1], v.at[0])
    get_rate = load(rate_hbm, rate)

    barrier = pltpu.get_barrier_semaphore()
    for who in ({"seq": nxt}, {"seq": prv}, {"head": side}, {"head": mirror}):
        pl.semaphore_signal(barrier, inc=1, device_id=who, device_id_type=MESH)

    get_q[0] = load(q_hbm.at[0], q.at[0])
    get_gain = load(gain_hbm, gain)
    get_ow = load(ow_hbm, ow)
    for t in range(1, ticks):
        get_k[t] = load(k_hbm.at[t + 1], k.at[t])
        get_v[t] = load(v_hbm.at[t + 1], v.at[t])
        get_q[t] = load(q_hbm.at[t], q.at[t])
    pl.semaphore_wait(barrier, 4)

    sent = []

    def remote(src, dst, ss, rs, who):
        return pltpu.make_async_remote_copy(
            src_ref=src, dst_ref=dst, send_sem=ss, recv_sem=rs, device_id=who, device_id_type=MESH
        )

    def push(copy):
        copy.start()
        sent.append(copy)

    step = rows // LATE_PIECES

    def near_copies(t):
        cuts = [(0, rows)] if t < last else [(i * step, (i + 1) * step) for i in reversed(range(LATE_PIECES))]
        found = []
        for j, (a, b) in enumerate(cuts):
            for i, hbm in enumerate((k_hbm, v_hbm)):
                at = (t, j, i)
                found.append(
                    remote(
                        hbm.at[t, pl.ds(a, b - a)], near.at[t, i, pl.ds(a, b - a)],
                        near_s.at[at], near_r.at[at], {"seq": nxt},
                    )
                )
        return found

    def send_near(t):
        for copy in near_copies(t):
            push(copy)

    def w_copy(t, i):
        return remote(w_send.at[t, i], w_recv.at[t, i], w_s.at[t, i], w_r.at[t, i], {"seq": nxt})

    def sv_of(t):
        column = jnp.broadcast_to(rate[t], (8, rows)).T[:, :1]
        return (column * v[t].astype(F32)).astype(BF16)

    def z_first(t, a, b, j, i):
        return remote(
            z_send.at[t, i, pl.ds(a, b - a)], z_recv.at[t, i, pl.ds(a, b - a)],
            z1_s.at[t, j, i], z1_r.at[t, j, i], {"head": first},
        )

    def z_second(t, a, b, j):
        return remote(
            z_fwd.at[t, pl.ds(a, b - a)], z_last.at[t, pl.ds(a, b - a)],
            z2_s.at[t, j], z2_r.at[t, j], {"head": second},
        )

    def project(combined, t, a, b, j):
        def piece(target):
            columns = pl.ds(pl.multiple_of(target * size, 128), size)
            return dot(combined, ow[:, columns]).astype(BF16)

        for i, target in enumerate((across, first)):
            z_send[t, i, a:b] = piece(target)
            push(z_first(t, a, b, j, i))
        z_keep[t, 0, a:b] = piece(second)
        z_keep[t, 1, a:b] = piece(h)

    def pass_on(t, a, b, j):
        z_first(t, a, b, j, 0).wait_recv()
        z_fwd[t, a:b] = (z_keep[t, 0, a:b].astype(F32) + z_recv[t, 0, a:b].astype(F32)).astype(BF16)
        z_second(t, a, b, j).start()
        z_first(t, a, b, j, 1).wait_recv()
        z_own[t, a:b] = z_keep[t, 1, a:b].astype(F32) + z_recv[t, 1, a:b].astype(F32)

    def finish(t, a, b, j):
        z_second(t, a, b, j).wait_recv()
        out_ref[t, a:b] = (z_own[t, a:b] + z_last[t, a:b].astype(F32)).astype(BF16)

    def waiting(copy, read):
        done = []

        def get():
            if not done:
                copy.wait()
                done.append(True)
            return read()

        return get

    def arrived(t, i):
        done = []

        def get():
            if not done:
                w_copy(t, i).wait_recv()
                done.append(True)
            return w_recv[t, i]

        return get

    own = [Rows(k.at[t], v.at[t]) for t in range(ticks)]
    prior = [Rows(near.at[t, 0], near.at[t, 1]) for t in range(ticks)]
    state = [waiting(get_w[i], lambda i=i: w[i]) for i in WEIGHTS]
    rounded = [lambda i=i: state[i]().astype(BF16) for i in WEIGHTS]
    send_near(0)

    for t in range(ticks):
        get_k[t].wait()
        get_v[t].wait()
        if t == 0:
            get_rate.wait()

        def update():
            def store(i, x):
                if t < last:
                    w_send[t, i] = x.astype(BF16)
                    push(w_copy(t, i))
                else:
                    new_ref[0, 0, i] = x

            fast_update(state, rounded, k[t], sv_of(t), store)
            if t < last:
                send_near(t + 1)

        def apply():
            get_q[t].wait()
            if t == 0:
                get_gain.wait()
            return normed_apply(rounded, q[t], gain[...])

        if t < last:
            update()
            normed = apply()
        else:
            normed = apply()
            update()
        if t == 0:
            get_ow.wait()
        scores_own = own_scores(q[t], own[t])
        if t < last:
            for copy in near_copies(t):
                copy.wait_recv()
            att = attend_rows(q[t], scores_own, prior[t], own[t], 0)
            project((att + normed).astype(BF16), t, 0, rows, 0)
            if t == 0:
                pl.when(odd == 0)(lambda: pass_on(0, 0, rows, 0))
            else:
                if t == 1:
                    pl.when(odd == 1)(lambda: pass_on(0, 0, rows, 0))
                finish(t - 1, 0, rows, 0)
                pass_on(t, 0, rows, 0)
            rounded = [arrived(t, i) for i in WEIGHTS]
            state = [lambda f=f: f().astype(F32) for f in rounded]
        else:
            cuts = [(i * step, (i + 1) * step) for i in reversed(range(LATE_PIECES))]
            copies = near_copies(t)
            for j, (a, b) in enumerate(cuts):
                for copy in copies[2 * j : 2 * j + 2]:
                    copy.wait_recv()
                att = attend_rows(q[t, a:b], scores_own[a:b], prior[t], own[t], a)
                project((att + normed[a:b]).astype(BF16), t, a, b, j)
                if j == 0:
                    finish(t - 1, 0, rows, 0)
                if j > 1:
                    pass_on(t, *cuts[j - 2], j - 2)
            for j in range(LATE_PIECES - 2, LATE_PIECES):
                pass_on(t, *cuts[j], j)
            for j, (a, b) in enumerate(cuts):
                finish(t, a, b, j)
    for copy in sent:
        copy.wait_send()
    for t in range(ticks):
        for j, (a, b) in enumerate(cuts if t == last else [(0, rows)]):
            z_second(t, a, b, j).wait_send()


def on_device(queries, key_vectors, values, learn_rates, norm_gain, out_weight, incoming):
    ticks, rows, size = queries.shape
    hbm = pl.BlockSpec(memory_space=pltpu.HBM)
    vmem = pl.BlockSpec(memory_space=pltpu.VMEM)
    dma = pltpu.SemaphoreType.DMA
    block = (ticks, rows, size)
    matrices = (len(WEIGHTS), size, size)
    scratch = [
        pltpu.VMEM(block, BF16),
        pltpu.VMEM(block, BF16),
        pltpu.VMEM(block, BF16),
        pltpu.VMEM((ticks, 1, rows), F32),
        pltpu.VMEM((1, size), F32),
        pltpu.VMEM(out_weight.shape, BF16),
        pltpu.VMEM(matrices, F32),
        pltpu.VMEM((ticks, 2, rows, size), BF16),
        pltpu.VMEM((ticks - 1, *matrices), BF16),
        pltpu.VMEM((ticks - 1, *matrices), BF16),
        pltpu.VMEM((ticks, 2, rows, size), BF16),
        pltpu.VMEM((ticks, 2, rows, size), BF16),
        pltpu.VMEM((ticks, 2, rows, size), BF16),
        pltpu.VMEM(block, BF16),
        pltpu.VMEM(block, BF16),
        pltpu.VMEM(block, F32),
        dma((6 + 3 * ticks,)),
        dma((ticks, LATE_PIECES, 2)),
        dma((ticks, LATE_PIECES, 2)),
        dma((ticks - 1, len(WEIGHTS))),
        dma((ticks - 1, len(WEIGHTS))),
        dma((ticks, LATE_PIECES, 2)),
        dma((ticks, LATE_PIECES, 2)),
        dma((ticks, LATE_PIECES)),
        dma((ticks, LATE_PIECES)),
    ]
    args = (
        queries, key_vectors, values, learn_rates.transpose(0, 2, 1), norm_gain.reshape(1, size),
        out_weight, incoming,
    )
    out, outgoing = pl.pallas_call(
        layer_kernel,
        out_shape=[
            jax.ShapeDtypeStruct(queries.shape, BF16),
            jax.ShapeDtypeStruct(incoming.shape, F32),
        ],
        in_specs=[hbm] * 7,
        out_specs=[vmem, vmem],
        scratch_shapes=scratch,
        compiler_params=pltpu.CompilerParams(
            collective_id=0, has_side_effects=True, vmem_limit_bytes=44 << 20
        ),
        name="layer_kernel",
    )(*(pltpu.with_memory_space_constraint(x, pltpu.HBM) for x in args))
    return out, outgoing


def solution(mesh):
    placed = (
        P(None, "seq", "head"),
        P(None, "seq", "head"),
        P(None, "seq", "head"),
        P(None, "seq", "head"),
        P("head"),
        P("head", None),
        P("seq", "head", None, None, None),
    )
    return jax.shard_map(
        on_device,
        mesh=mesh,
        in_specs=placed,
        out_specs=(P(None, "seq", "head"), P("seq", "head", None, None, None)),
        check_vma=False,
    )
```

```python
import functools

import jax
import jax.numpy as jnp
from jax import lax
from jax.experimental import pallas as pl
from jax.experimental.pallas import tpu as pltpu
from jax.sharding import PartitionSpec as P


F32, BF16 = jnp.float32, jnp.bfloat16
MESH = pl.DeviceIdType.MESH
WEIGHTS = (0, 1, 2)
LATE_PIECES = 4
LANES = 128


def dot(a, b, over=(1, 0)):
    return lax.dot_general(a, b, (((over[0],), (over[1],)), ((), ())), preferred_element_type=F32)


def normed_apply(rounded, query_rows, gain_row):
    first_proj = dot(query_rows, rounded[0]())
    third_proj = dot(query_rows, rounded[1]())
    hidden = (first_proj * jax.nn.sigmoid(first_proj) * third_proj).astype(BF16)
    fast_out = dot(hidden, rounded[2]())
    mean_sq = jnp.mean(fast_out * fast_out, axis=1, keepdims=True)
    return fast_out * lax.rsqrt(mean_sq + 1e-06) * gain_row


def fast_update(olds, rounded, key_rows, scaled_values, put_new):
    first_proj = dot(key_rows, rounded[0]())
    third_proj = dot(key_rows, rounded[1]())
    gate_sig = jax.nn.sigmoid(first_proj)
    gated = first_proj * gate_sig

    def put(i, grad):
        old = olds[i]()
        stepped = old + grad
        before_sq = jnp.mean(old * old, axis=0, keepdims=True)
        after_sq = jnp.mean(stepped * stepped, axis=0, keepdims=True)
        put_new(i, stepped * jnp.sqrt((before_sq + 1e-06) / (after_sq + 1e-06)))

    back_grad = dot(scaled_values, rounded[2](), (1, 1))
    slope = gate_sig * (1.0 + first_proj * (1.0 - gate_sig))
    put(0, dot(key_rows, (back_grad * third_proj * slope).astype(BF16), (0, 0)))
    put(1, dot(key_rows, (back_grad * gated).astype(BF16), (0, 0)))
    hidden = (gated * third_proj).astype(BF16)
    put(2, dot(hidden, scaled_values, (0, 0)))


def softmax_parts(scores, own):
    expo = jnp.exp(scores - jnp.max(scores, axis=1, keepdims=True))
    probs = expo / jnp.sum(expo, axis=1, keepdims=True)
    zero = jnp.zeros_like(probs)
    return jnp.where(own, probs, zero).astype(BF16), jnp.where(own, zero, probs).astype(BF16)


def own_scores(query_rows, own):
    return dot(query_rows, own.keys(0, own.length), (1, 1))


def attend_rows(query_rows, scores_own, prior, own, low):
    span, size = query_rows.shape
    length = own.length
    reach = min(length, -(-(low + span) // LANES) * LANES)

    def joined(part_own, part_prior):
        if not low:
            return part_prior(0, length)
        return jnp.concatenate([part_own(0, low), part_prior(low, length)], axis=0)

    row = lax.broadcasted_iota(jnp.int32, (span, length), 0) + low
    is_own = lax.broadcasted_iota(jnp.int32, (span, length), 1) <= row
    other = dot(query_rows, joined(own.keys, prior.keys), (1, 1))
    scores = jnp.where(is_own, scores_own, other) * size ** (-0.5)
    own_probs, prior_probs = softmax_parts(scores, is_own)
    return dot(own_probs[:, :reach], own.values(0, reach)) + dot(
        prior_probs, joined(own.values, prior.values)
    )


class Rows:
    def __init__(self, keys_ref, values_ref):
        self.k, self.v, self.length = keys_ref, values_ref, keys_ref.shape[0]

    def keys(self, a, b):
        return self.k[a:b]

    def values(self, a, b):
        return self.v[a:b]


def layer_kernel(
    q_hbm, k_hbm, v_hbm, rate_hbm, gain_hbm, ow_hbm, w_hbm,
    out_ref, new_ref,
    q, k, v, rate, gain, ow, w,
    near, w_send, w_recv, z_send, z_recv, z_keep, z_fwd, z_last, z_own, out, new,
    in_sem, out_sem, near_s, near_r, w_s, w_r, z1_s, z1_r, z2_s, z2_r,
):
    ticks, rows, size = q.shape
    last = ticks - 1
    n_seq, n_head = lax.axis_size("seq"), lax.axis_size("head")
    s, h = lax.axis_index("seq"), lax.axis_index("head")
    nxt, prv = lax.rem(s + 1, n_seq), lax.rem(s + n_seq - 1, n_seq)
    odd = lax.rem(s, 2)
    side = h + 1 - 2 * lax.rem(h, 2)
    mirror = n_head - 1 - h
    across = lax.rem(h + n_head // 2, n_head)
    first, second = side, mirror

    loads = []

    def load(src, dst):
        copy = pltpu.make_async_copy(src, dst, in_sem.at[len(loads)])
        copy.start()
        loads.append(copy)
        return copy

    get_k = [None] * ticks
    get_v = [None] * ticks
    get_q = [None] * ticks
    get_k[0] = load(k_hbm.at[1], k.at[0])
    get_w = [load(w_hbm.at[0, 0, i], w.at[i]) for i in WEIGHTS]
    get_v[0] = load(v_hbm.at[1], v.at[0])
    get_rate = load(rate_hbm, rate)

    barrier = pltpu.get_barrier_semaphore()
    for who in ({"seq": nxt}, {"seq": prv}, {"head": side}, {"head": mirror}):
        pl.semaphore_signal(barrier, inc=1, device_id=who, device_id_type=MESH)

    get_q[0] = load(q_hbm.at[0], q.at[0])
    get_gain = load(gain_hbm, gain)
    get_ow = load(ow_hbm, ow)
    for t in range(1, ticks):
        get_k[t] = load(k_hbm.at[t + 1], k.at[t])
        get_v[t] = load(v_hbm.at[t + 1], v.at[t])
        get_q[t] = load(q_hbm.at[t], q.at[t])
    pl.semaphore_wait(barrier, 4)

    sent = []

    def remote(src, dst, ss, rs, who):
        return pltpu.make_async_remote_copy(
            src_ref=src, dst_ref=dst, send_sem=ss, recv_sem=rs, device_id=who, device_id_type=MESH
        )

    def push(copy):
        copy.start()
        sent.append(copy)

    step = rows // LATE_PIECES
    cuts = [(i * step, (i + 1) * step) for i in reversed(range(LATE_PIECES))]
    leaving = []

    def leave(src, dst):
        copy = pltpu.make_async_copy(src, dst, out_sem.at[len(leaving)])
        copy.start()
        leaving.append(copy)

    def near_copies(t):
        found = []
        for j, (a, b) in enumerate(cuts if t == last else [(0, rows)]):
            for i, hbm in enumerate((k_hbm, v_hbm)):
                at = (t, j, i)
                found.append(
                    remote(
                        hbm.at[t, pl.ds(a, b - a)], near.at[t, i, pl.ds(a, b - a)],
                        near_s.at[at], near_r.at[at], {"seq": nxt},
                    )
                )
        return found

    def send_near(t):
        for copy in near_copies(t):
            push(copy)

    def w_copy(t, i):
        return remote(w_send.at[t, i], w_recv.at[t, i], w_s.at[t, i], w_r.at[t, i], {"seq": nxt})

    def sv_of(t):
        column = jnp.broadcast_to(rate[t], (8, rows)).T[:, :1]
        return (column * v[t].astype(F32)).astype(BF16)

    def z_first(t, a, b, j, i):
        return remote(
            z_send.at[t, i, pl.ds(a, b - a)], z_recv.at[t, i, pl.ds(a, b - a)],
            z1_s.at[t, j, i], z1_r.at[t, j, i], {"head": first},
        )

    def z_second(t, a, b, j):
        return remote(
            z_fwd.at[t, pl.ds(a, b - a)], z_last.at[t, pl.ds(a, b - a)],
            z2_s.at[t, j], z2_r.at[t, j], {"head": second},
        )

    def project(combined, t, a, b, j):
        def piece(target):
            columns = pl.ds(pl.multiple_of(target * size, 128), size)
            return dot(combined, ow[:, columns]).astype(BF16)

        for i, target in enumerate((across, first)):
            z_send[t, i, a:b] = piece(target)
            push(z_first(t, a, b, j, i))
        z_keep[t, 0, a:b] = piece(second)
        z_keep[t, 1, a:b] = piece(h)

    def pass_on(t, a, b, j):
        z_first(t, a, b, j, 0).wait_recv()
        z_fwd[t, a:b] = (z_keep[t, 0, a:b].astype(F32) + z_recv[t, 0, a:b].astype(F32)).astype(BF16)
        z_second(t, a, b, j).start()
        z_first(t, a, b, j, 1).wait_recv()
        z_own[t, a:b] = z_keep[t, 1, a:b].astype(F32) + z_recv[t, 1, a:b].astype(F32)

    def finish(t, a, b, j):
        z_second(t, a, b, j).wait_recv()
        out[t, a:b] = (z_own[t, a:b] + z_last[t, a:b].astype(F32)).astype(BF16)
        piece = pl.ds(a, b - a)
        leave(out.at[t, piece], out_ref.at[t, piece])

    def waiting(copy, read):
        done = []

        def get():
            if not done:
                copy.wait()
                done.append(True)
            return read()

        return get

    def arrived(t, i):
        done = []

        def get():
            if not done:
                w_copy(t, i).wait_recv()
                done.append(True)
            return w_recv[t, i]

        return get

    own = [Rows(k.at[t], v.at[t]) for t in range(ticks)]
    prior = [Rows(near.at[t, 0], near.at[t, 1]) for t in range(ticks)]
    state = [waiting(get_w[i], lambda i=i: w[i]) for i in WEIGHTS]
    rounded = [lambda i=i: state[i]().astype(BF16) for i in WEIGHTS]
    send_near(0)

    for t in range(ticks):
        get_k[t].wait()
        get_v[t].wait()
        if t == 0:
            get_rate.wait()

        def update():
            def store(i, x):
                if t < last:
                    w_send[t, i] = x.astype(BF16)
                    push(w_copy(t, i))
                else:
                    new[i] = x
                    leave(new.at[i], new_ref.at[0, 0, i])

            fast_update(state, rounded, k[t], sv_of(t), store)
            if t < last:
                send_near(t + 1)

        def apply():
            get_q[t].wait()
            if t == 0:
                get_gain.wait()
            return normed_apply(rounded, q[t], gain[...])

        if t < last:
            update()
        normed = apply()
        if t == 0:
            get_ow.wait()
        scores_own = own_scores(q[t], own[t])
        if t < last:
            if t == 1:
                pl.when(odd == 0)(lambda: pass_on(0, 0, rows, 0))
            for copy in near_copies(t):
                copy.wait_recv()
            att = attend_rows(q[t], scores_own, prior[t], own[t], 0)
            project((att + normed).astype(BF16), t, 0, rows, 0)
            if t == 1:
                pl.when(odd == 1)(lambda: pass_on(0, 0, rows, 0))
            rounded = [arrived(t, i) for i in WEIGHTS]
            state = [lambda f=f: f().astype(F32) for f in rounded]
        else:
            copies = near_copies(t)
            for j, (a, b) in enumerate(cuts):
                for copy in copies[2 * j : 2 * j + 2]:
                    copy.wait_recv()
                att = attend_rows(q[t, a:b], scores_own[a:b], prior[t], own[t], a)
                project((att + normed[a:b]).astype(BF16), t, a, b, j)
                if j == 0:
                    for early in range(1, last):
                        pass_on(early, 0, rows, 0)
            update()
            for early in range(last):
                finish(early, 0, rows, 0)
            for j, (a, b) in enumerate(cuts):
                pass_on(t, a, b, j)
            for j, (a, b) in enumerate(cuts):
                finish(t, a, b, j)
    for copy in leaving:
        copy.wait()
    for copy in sent:
        copy.wait_send()
    for t in range(ticks):
        for j, (a, b) in enumerate(cuts if t == last else [(0, rows)]):
            z_second(t, a, b, j).wait_send()


def write_kernel(out_ref, new_ref, out_to, new_to, sem):
    pairs = [(new_ref.at[0, 0, i], new_to.at[0, 0, i]) for i in range(new_ref.shape[2])]
    pairs += [(out_ref.at[t], out_to.at[t]) for t in range(out_ref.shape[0])]
    copies = [pltpu.make_async_copy(a, b, sem.at[i]) for i, (a, b) in enumerate(pairs)]
    for copy in copies:
        copy.start()
    for copy in copies:
        copy.wait()


def on_device(queries, key_vectors, values, learn_rates, norm_gain, out_weight, incoming):
    ticks, rows, size = queries.shape
    hbm = pl.BlockSpec(memory_space=pltpu.HBM)
    anywhere = pl.BlockSpec(memory_space=pl.ANY)
    dma = pltpu.SemaphoreType.DMA
    block = (ticks, rows, size)
    matrices = (len(WEIGHTS), size, size)
    scratch = [
        pltpu.VMEM(block, BF16),
        pltpu.VMEM(block, BF16),
        pltpu.VMEM(block, BF16),
        pltpu.VMEM((ticks, 1, rows), F32),
        pltpu.VMEM((1, size), F32),
        pltpu.VMEM(out_weight.shape, BF16),
        pltpu.VMEM(matrices, F32),
        pltpu.VMEM((ticks, 2, rows, size), BF16),
        pltpu.VMEM((ticks - 1, *matrices), BF16),
        pltpu.VMEM((ticks - 1, *matrices), BF16),
        pltpu.VMEM((ticks, 2, rows, size), BF16),
        pltpu.VMEM((ticks, 2, rows, size), BF16),
        pltpu.VMEM((ticks, 2, rows, size), BF16),
        pltpu.VMEM(block, BF16),
        pltpu.VMEM(block, BF16),
        pltpu.VMEM(block, F32),
        pltpu.VMEM(block, BF16),
        pltpu.VMEM(matrices, F32),
        dma((6 + 3 * ticks,)),
        dma((len(WEIGHTS) + ticks - 1 + LATE_PIECES,)),
        dma((ticks, LATE_PIECES, 2)),
        dma((ticks, LATE_PIECES, 2)),
        dma((ticks - 1, len(WEIGHTS))),
        dma((ticks - 1, len(WEIGHTS))),
        dma((ticks, LATE_PIECES, 2)),
        dma((ticks, LATE_PIECES, 2)),
        dma((ticks, LATE_PIECES)),
        dma((ticks, LATE_PIECES)),
    ]
    args = (
        queries, key_vectors, values, learn_rates.transpose(0, 2, 1), norm_gain.reshape(1, size),
        out_weight, incoming,
    )
    out, outgoing = pl.pallas_call(
        layer_kernel,
        out_shape=[
            jax.ShapeDtypeStruct(queries.shape, BF16),
            jax.ShapeDtypeStruct(incoming.shape, F32),
        ],
        in_specs=[hbm] * 7,
        out_specs=[anywhere, anywhere],
        scratch_shapes=scratch,
        compiler_params=pltpu.CompilerParams(
            collective_id=0, has_side_effects=True, vmem_limit_bytes=44 << 20
        ),
        name="layer_kernel",
    )(*(pltpu.with_memory_space_constraint(x, pltpu.HBM) for x in args))
    return pl.pallas_call(
        write_kernel,
        out_shape=[jax.ShapeDtypeStruct(x.shape, x.dtype) for x in (out, outgoing)],
        in_specs=[anywhere, anywhere],
        out_specs=[anywhere, anywhere],
        scratch_shapes=[dma((ticks + len(WEIGHTS),))],
        compiler_params=pltpu.CompilerParams(vmem_limit_bytes=1 << 20),
        name="write_kernel",
    )(out, outgoing)


def solution(mesh):
    placed = (
        P(None, "seq", "head"),
        P(None, "seq", "head"),
        P(None, "seq", "head"),
        P(None, "seq", "head"),
        P("head"),
        P("head", None),
        P("seq", "head", None, None, None),
    )
    return jax.shard_map(
        on_device,
        mesh=mesh,
        in_specs=placed,
        out_specs=(P(None, "seq", "head"), P("seq", "head", None, None, None)),
        check_vma=False,
    )
```

```python
import functools

import jax
import jax.numpy as jnp
from jax import lax
from jax.experimental import pallas as pl
from jax.experimental.pallas import tpu as pltpu
from jax.sharding import PartitionSpec as P


F32, BF16 = jnp.float32, jnp.bfloat16
MESH = pl.DeviceIdType.MESH
WEIGHTS = (0, 1, 2)
LATE_PIECES = 4
LANES = 128


def dot(a, b, over=(1, 0)):
    return lax.dot_general(a, b, (((over[0],), (over[1],)), ((), ())), preferred_element_type=F32)


def normed_apply(rounded, query_rows, gain_row):
    first_proj = dot(query_rows, rounded[0]())
    third_proj = dot(query_rows, rounded[1]())
    hidden = (first_proj * jax.nn.sigmoid(first_proj) * third_proj).astype(BF16)
    fast_out = dot(hidden, rounded[2]())
    mean_sq = jnp.mean(fast_out * fast_out, axis=1, keepdims=True)
    return fast_out * lax.rsqrt(mean_sq + 1e-06) * gain_row


def fast_update(olds, rounded, key_rows, scaled_values, put_new):
    first_proj = dot(key_rows, rounded[0]())
    third_proj = dot(key_rows, rounded[1]())
    gate_sig = jax.nn.sigmoid(first_proj)
    gated = first_proj * gate_sig

    def put(i, grad):
        old = olds[i]()
        stepped = old + grad
        before_sq = jnp.mean(old * old, axis=0, keepdims=True)
        after_sq = jnp.mean(stepped * stepped, axis=0, keepdims=True)
        put_new(i, stepped * jnp.sqrt((before_sq + 1e-06) / (after_sq + 1e-06)))

    back_grad = dot(scaled_values, rounded[2](), (1, 1))
    slope = gate_sig * (1.0 + first_proj * (1.0 - gate_sig))
    put(0, dot(key_rows, (back_grad * third_proj * slope).astype(BF16), (0, 0)))
    put(1, dot(key_rows, (back_grad * gated).astype(BF16), (0, 0)))
    hidden = (gated * third_proj).astype(BF16)
    put(2, dot(hidden, scaled_values, (0, 0)))


def softmax_parts(scores, own):
    expo = jnp.exp(scores - jnp.max(scores, axis=1, keepdims=True))
    probs = expo / jnp.sum(expo, axis=1, keepdims=True)
    zero = jnp.zeros_like(probs)
    return jnp.where(own, probs, zero).astype(BF16), jnp.where(own, zero, probs).astype(BF16)


def own_scores(query_rows, own):
    return dot(query_rows, own.keys(0, own.length), (1, 1))


def attend_rows(query_rows, scores_own, prior, own, low):
    span, size = query_rows.shape
    length = own.length
    reach = min(length, -(-(low + span) // LANES) * LANES)

    def joined(part_own, part_prior):
        if not low:
            return part_prior(0, length)
        return jnp.concatenate([part_own(0, low), part_prior(low, length)], axis=0)

    row = lax.broadcasted_iota(jnp.int32, (span, length), 0) + low
    is_own = lax.broadcasted_iota(jnp.int32, (span, length), 1) <= row
    other = dot(query_rows, joined(own.keys, prior.keys), (1, 1))
    scores = jnp.where(is_own, scores_own, other) * size ** (-0.5)
    own_probs, prior_probs = softmax_parts(scores, is_own)
    return dot(own_probs[:, :reach], own.values(0, reach)) + dot(
        prior_probs, joined(own.values, prior.values)
    )


class Rows:
    def __init__(self, keys_ref, values_ref):
        self.k, self.v, self.length = keys_ref, values_ref, keys_ref.shape[0]

    def keys(self, a, b):
        return self.k[a:b]

    def values(self, a, b):
        return self.v[a:b]


def layer_kernel(
    q_hbm, k_hbm, v_hbm, rate_hbm, gain_hbm, ow_hbm, w_hbm,
    out_ref, new_ref,
    q, k, v, rate, gain, ow, w,
    near, w_send, w_recv, z_send, z_recv, z_keep, z_fwd, z_last, out, new,
    in_sem, out_sem, near_s, near_r, w_s, w_r, z1_s, z1_r, z2_s, z2_r,
):
    ticks, rows, size = q.shape
    last = ticks - 1
    n_seq, n_head = lax.axis_size("seq"), lax.axis_size("head")
    s, h = lax.axis_index("seq"), lax.axis_index("head")
    nxt, prv = lax.rem(s + 1, n_seq), lax.rem(s + n_seq - 1, n_seq)
    odd = lax.rem(s, 2)
    side = h + 1 - 2 * lax.rem(h, 2)
    mirror = n_head - 1 - h
    across = lax.rem(h + n_head // 2, n_head)
    first, second = side, mirror

    loads = []

    def load(src, dst):
        copy = pltpu.make_async_copy(src, dst, in_sem.at[len(loads)])
        copy.start()
        loads.append(copy)
        return copy

    get_k = [None] * ticks
    get_v = [None] * ticks
    get_q = [None] * ticks
    get_k[0] = load(k_hbm.at[1], k.at[0])
    get_w = [load(w_hbm.at[0, 0, i], w.at[i]) for i in WEIGHTS]
    get_v[0] = load(v_hbm.at[1], v.at[0])
    get_rate = load(rate_hbm, rate)

    barrier = pltpu.get_barrier_semaphore()
    for who in ({"seq": nxt}, {"seq": prv}, {"head": side}, {"head": mirror}):
        pl.semaphore_signal(barrier, inc=1, device_id=who, device_id_type=MESH)

    get_q[0] = load(q_hbm.at[0], q.at[0])
    get_gain = load(gain_hbm, gain)
    get_ow = load(ow_hbm, ow)
    for t in range(1, ticks):
        get_k[t] = load(k_hbm.at[t + 1], k.at[t])
        get_v[t] = load(v_hbm.at[t + 1], v.at[t])
        get_q[t] = load(q_hbm.at[t], q.at[t])
    pl.semaphore_wait(barrier, 4)

    sent = []

    def remote(src, dst, ss, rs, who):
        return pltpu.make_async_remote_copy(
            src_ref=src, dst_ref=dst, send_sem=ss, recv_sem=rs, device_id=who, device_id_type=MESH
        )

    def push(copy):
        copy.start()
        sent.append(copy)

    step = rows // LATE_PIECES
    cuts = [(i * step, (i + 1) * step) for i in reversed(range(LATE_PIECES))]
    half = LATE_PIECES // 2
    leaving = []

    def leave(src, dst):
        copy = pltpu.make_async_copy(src, dst, out_sem.at[len(leaving)])
        copy.start()
        leaving.append(copy)

    def near_copies(t):
        found = []
        for j, (a, b) in enumerate(cuts if t == last else [(0, rows)]):
            for i, hbm in enumerate((k_hbm, v_hbm)):
                at = (t, j, i)
                found.append(
                    remote(
                        hbm.at[t, pl.ds(a, b - a)], near.at[t, i, pl.ds(a, b - a)],
                        near_s.at[at], near_r.at[at], {"seq": nxt},
                    )
                )
        return found

    def send_near(t):
        for copy in near_copies(t):
            push(copy)

    def w_copy(t, i):
        return remote(w_send.at[t, i], w_recv.at[t, i], w_s.at[t, i], w_r.at[t, i], {"seq": nxt})

    def sv_of(t):
        column = jnp.broadcast_to(rate[t], (8, rows)).T[:, :1]
        return (column * v[t].astype(F32)).astype(BF16)

    def z_first(t, a, b, j, i):
        return remote(
            z_send.at[t, i, pl.ds(a, b - a)], z_recv.at[t, i, pl.ds(a, b - a)],
            z1_s.at[t, j, i], z1_r.at[t, j, i], {"head": first},
        )

    def z_second(t, a, b, j):
        return remote(
            z_fwd.at[t, pl.ds(a, b - a)], z_last.at[t, pl.ds(a, b - a)],
            z2_s.at[t, j], z2_r.at[t, j], {"head": second},
        )

    def project(combined, t, a, b, j):
        def piece(target):
            columns = pl.ds(pl.multiple_of(target * size, 128), size)
            return dot(combined, ow[:, columns]).astype(BF16)

        for i, target in enumerate((across, first)):
            z_send[t, i, a:b] = piece(target)
            push(z_first(t, a, b, j, i))
        z_keep[t, 0, a:b] = piece(second)
        z_keep[t, 1, a:b] = piece(h)

    def pass_on(t, a, b, j):
        z_first(t, a, b, j, 0).wait_recv()
        z_fwd[t, a:b] = (z_keep[t, 0, a:b].astype(F32) + z_recv[t, 0, a:b].astype(F32)).astype(BF16)
        z_second(t, a, b, j).start()

    def finish(t, a, b, j):
        z_first(t, a, b, j, 1).wait_recv()
        z_second(t, a, b, j).wait_recv()
        pair = z_keep[t, 1, a:b].astype(F32) + z_recv[t, 1, a:b].astype(F32)
        out[t, a:b] = (pair + z_last[t, a:b].astype(F32)).astype(BF16)
        piece = pl.ds(a, b - a)
        leave(out.at[t, piece], out_ref.at[t, piece])

    def waiting(copy, read):
        done = []

        def get():
            if not done:
                copy.wait()
                done.append(True)
            return read()

        return get

    def arrived(t, i):
        done = []

        def get():
            if not done:
                w_copy(t, i).wait_recv()
                done.append(True)
            return w_recv[t, i]

        return get

    own = [Rows(k.at[t], v.at[t]) for t in range(ticks)]
    prior = [Rows(near.at[t, 0], near.at[t, 1]) for t in range(ticks)]
    state = [waiting(get_w[i], lambda i=i: w[i]) for i in WEIGHTS]
    rounded = [lambda i=i: state[i]().astype(BF16) for i in WEIGHTS]
    send_near(0)

    for t in range(ticks):
        get_k[t].wait()
        get_v[t].wait()
        if t == 0:
            get_rate.wait()

        def update():
            def store(i, x):
                if t < last:
                    w_send[t, i] = x.astype(BF16)
                    push(w_copy(t, i))
                else:
                    new[i] = x
                    leave(new.at[i], new_ref.at[0, 0, i])
                    if i == 1:
                        pass_on(t, *cuts[half], half)

            fast_update(state, rounded, k[t], sv_of(t), store)
            if t < last:
                send_near(t + 1)

        def apply():
            get_q[t].wait()
            if t == 0:
                get_gain.wait()
            return normed_apply(rounded, q[t], gain[...])

        if t == 1:
            pl.when(odd == 0)(lambda: pass_on(0, 0, rows, 0))
        if t < last:
            update()
        normed = apply()
        if t == 0:
            get_ow.wait()
        scores_own = own_scores(q[t], own[t])
        if t < last:
            for copy in near_copies(t):
                copy.wait_recv()
            att = attend_rows(q[t], scores_own, prior[t], own[t], 0)
            project((att + normed).astype(BF16), t, 0, rows, 0)
            if t == 1:
                pl.when(odd == 1)(lambda: pass_on(0, 0, rows, 0))
            if t:
                pass_on(t, 0, rows, 0)
            rounded = [arrived(t, i) for i in WEIGHTS]
            state = [lambda f=f: f().astype(F32) for f in rounded]
        else:
            copies = near_copies(t)
            for j, (a, b) in enumerate(cuts):
                for copy in copies[2 * j : 2 * j + 2]:
                    copy.wait_recv()
                att = attend_rows(q[t, a:b], scores_own[a:b], prior[t], own[t], a)
                project((att + normed[a:b]).astype(BF16), t, a, b, j)
            for j in range(half):
                pass_on(t, *cuts[j], j)
            update()
            for j in range(half + 1, LATE_PIECES):
                pass_on(t, *cuts[j], j)
            for early in range(last):
                finish(early, 0, rows, 0)
            for j, (a, b) in enumerate(cuts):
                finish(t, a, b, j)
    for copy in leaving:
        copy.wait()
    for copy in sent:
        copy.wait_send()
    for t in range(ticks):
        for j, (a, b) in enumerate(cuts if t == last else [(0, rows)]):
            z_second(t, a, b, j).wait_send()


def write_kernel(out_ref, new_ref, out_to, new_to, sem):
    pairs = [(new_ref.at[0, 0, i], new_to.at[0, 0, i]) for i in range(new_ref.shape[2])]
    pairs += [(out_ref.at[t], out_to.at[t]) for t in range(out_ref.shape[0])]
    copies = [pltpu.make_async_copy(a, b, sem.at[i]) for i, (a, b) in enumerate(pairs)]
    for copy in copies:
        copy.start()
    for copy in copies:
        copy.wait()


def on_device(queries, key_vectors, values, learn_rates, norm_gain, out_weight, incoming):
    ticks, rows, size = queries.shape
    hbm = pl.BlockSpec(memory_space=pltpu.HBM)
    anywhere = pl.BlockSpec(memory_space=pl.ANY)
    dma = pltpu.SemaphoreType.DMA
    block = (ticks, rows, size)
    matrices = (len(WEIGHTS), size, size)
    scratch = [
        pltpu.VMEM(block, BF16),
        pltpu.VMEM(block, BF16),
        pltpu.VMEM(block, BF16),
        pltpu.VMEM((ticks, 1, rows), F32),
        pltpu.VMEM((1, size), F32),
        pltpu.VMEM(out_weight.shape, BF16),
        pltpu.VMEM(matrices, F32),
        pltpu.VMEM((ticks, 2, rows, size), BF16),
        pltpu.VMEM((ticks - 1, *matrices), BF16),
        pltpu.VMEM((ticks - 1, *matrices), BF16),
        pltpu.VMEM((ticks, 2, rows, size), BF16),
        pltpu.VMEM((ticks, 2, rows, size), BF16),
        pltpu.VMEM((ticks, 2, rows, size), BF16),
        pltpu.VMEM(block, BF16),
        pltpu.VMEM(block, BF16),
        pltpu.VMEM(block, BF16),
        pltpu.VMEM(matrices, F32),
        dma((6 + 3 * ticks,)),
        dma((len(WEIGHTS) + ticks - 1 + LATE_PIECES,)),
        dma((ticks, LATE_PIECES, 2)),
        dma((ticks, LATE_PIECES, 2)),
        dma((ticks - 1, len(WEIGHTS))),
        dma((ticks - 1, len(WEIGHTS))),
        dma((ticks, LATE_PIECES, 2)),
        dma((ticks, LATE_PIECES, 2)),
        dma((ticks, LATE_PIECES)),
        dma((ticks, LATE_PIECES)),
    ]
    args = (
        queries, key_vectors, values, learn_rates.transpose(0, 2, 1), norm_gain.reshape(1, size),
        out_weight, incoming,
    )
    out, outgoing = pl.pallas_call(
        layer_kernel,
        out_shape=[
            jax.ShapeDtypeStruct(queries.shape, BF16),
            jax.ShapeDtypeStruct(incoming.shape, F32),
        ],
        in_specs=[hbm] * 7,
        out_specs=[anywhere, anywhere],
        scratch_shapes=scratch,
        compiler_params=pltpu.CompilerParams(
            collective_id=0, has_side_effects=True, vmem_limit_bytes=44 << 20
        ),
        name="layer_kernel",
    )(*(pltpu.with_memory_space_constraint(x, pltpu.HBM) for x in args))
    return pl.pallas_call(
        write_kernel,
        out_shape=[jax.ShapeDtypeStruct(x.shape, x.dtype) for x in (out, outgoing)],
        in_specs=[anywhere, anywhere],
        out_specs=[anywhere, anywhere],
        scratch_shapes=[dma((ticks + len(WEIGHTS),))],
        compiler_params=pltpu.CompilerParams(vmem_limit_bytes=1 << 20),
        name="write_kernel",
    )(out, outgoing)


def solution(mesh):
    placed = (
        P(None, "seq", "head"),
        P(None, "seq", "head"),
        P(None, "seq", "head"),
        P(None, "seq", "head"),
        P("head"),
        P("head", None),
        P("seq", "head", None, None, None),
    )
    return jax.shard_map(
        on_device,
        mesh=mesh,
        in_specs=placed,
        out_specs=(P(None, "seq", "head"), P("seq", "head", None, None, None)),
        check_vma=False,
    )
```

```python
import functools

import jax
import jax.numpy as jnp
from jax import lax
from jax.experimental import pallas as pl
from jax.experimental.pallas import tpu as pltpu
from jax.sharding import PartitionSpec as P


F32, BF16 = jnp.float32, jnp.bfloat16
MESH = pl.DeviceIdType.MESH
WEIGHTS = (0, 1, 2)
LATE_PIECES = 4
LANES = 128


def dot(a, b, over=(1, 0)):
    return lax.dot_general(a, b, (((over[0],), (over[1],)), ((), ())), preferred_element_type=F32)


def normed_apply(rounded, query_rows, gain_row):
    first_proj = dot(query_rows, rounded[0]())
    third_proj = dot(query_rows, rounded[1]())
    hidden = (first_proj * jax.nn.sigmoid(first_proj) * third_proj).astype(BF16)
    fast_out = dot(hidden, rounded[2]())
    mean_sq = jnp.mean(fast_out * fast_out, axis=1, keepdims=True)
    return fast_out * lax.rsqrt(mean_sq + 1e-06) * gain_row


def fast_update(olds, rounded, key_rows, scaled_values, put_new):
    first_proj = dot(key_rows, rounded[0]())
    third_proj = dot(key_rows, rounded[1]())
    gate_sig = jax.nn.sigmoid(first_proj)
    gated = first_proj * gate_sig

    def put(i, grad):
        old = olds[i]()
        stepped = old + grad
        before_sq = jnp.mean(old * old, axis=0, keepdims=True)
        after_sq = jnp.mean(stepped * stepped, axis=0, keepdims=True)
        put_new(i, stepped * jnp.sqrt((before_sq + 1e-06) / (after_sq + 1e-06)))

    back_grad = dot(scaled_values, rounded[2](), (1, 1))
    slope = gate_sig * (1.0 + first_proj * (1.0 - gate_sig))
    put(0, dot(key_rows, (back_grad * third_proj * slope).astype(BF16), (0, 0)))
    put(1, dot(key_rows, (back_grad * gated).astype(BF16), (0, 0)))
    hidden = (gated * third_proj).astype(BF16)
    put(2, dot(hidden, scaled_values, (0, 0)))


def softmax_parts(scores, own):
    expo = jnp.exp(scores - jnp.max(scores, axis=1, keepdims=True))
    probs = expo / jnp.sum(expo, axis=1, keepdims=True)
    zero = jnp.zeros_like(probs)
    return jnp.where(own, probs, zero).astype(BF16), jnp.where(own, zero, probs).astype(BF16)


def own_scores(query_rows, own):
    return dot(query_rows, own.keys(0, own.length), (1, 1))


def attend_rows(query_rows, scores_own, prior, own, low):
    span, size = query_rows.shape
    length = own.length
    reach = min(length, -(-(low + span) // LANES) * LANES)

    def joined(part_own, part_prior):
        if not low:
            return part_prior(0, length)
        return jnp.concatenate([part_own(0, low), part_prior(low, length)], axis=0)

    row = lax.broadcasted_iota(jnp.int32, (span, length), 0) + low
    is_own = lax.broadcasted_iota(jnp.int32, (span, length), 1) <= row
    other = dot(query_rows, joined(own.keys, prior.keys), (1, 1))
    scores = jnp.where(is_own, scores_own, other) * size ** (-0.5)
    own_probs, prior_probs = softmax_parts(scores, is_own)
    return dot(own_probs[:, :reach], own.values(0, reach)) + dot(
        prior_probs, joined(own.values, prior.values)
    )


class Rows:
    def __init__(self, keys_ref, values_ref):
        self.k, self.v, self.length = keys_ref, values_ref, keys_ref.shape[0]

    def keys(self, a, b):
        return self.k[a:b]

    def values(self, a, b):
        return self.v[a:b]


def layer_kernel(
    q_hbm, k_hbm, v_hbm, rate_hbm, gain_hbm, ow_hbm, w_hbm,
    out_ref, new_ref,
    q, k, v, rate, gain, ow, w,
    near, w_send, w_recv, z_send, z_recv, z_keep, z_fwd, z_last, out, new,
    in_sem, near_s, near_r, w_s, w_r, z1_s, z1_r, z2_s, z2_r,
):
    ticks, rows, size = q.shape
    last = ticks - 1
    n_seq, n_head = lax.axis_size("seq"), lax.axis_size("head")
    s, h = lax.axis_index("seq"), lax.axis_index("head")
    nxt, prv = lax.rem(s + 1, n_seq), lax.rem(s + n_seq - 1, n_seq)
    odd = lax.rem(s, 2)
    side = h + 1 - 2 * lax.rem(h, 2)
    mirror = n_head - 1 - h
    across = lax.rem(h + n_head // 2, n_head)
    first, second = side, mirror

    loads = []

    def load(src, dst):
        copy = pltpu.make_async_copy(src, dst, in_sem.at[len(loads)])
        copy.start()
        loads.append(copy)
        return copy

    get_k = [None] * ticks
    get_v = [None] * ticks
    get_q = [None] * ticks
    get_k[0] = load(k_hbm.at[1], k.at[0])
    get_w = [load(w_hbm.at[0, 0, i], w.at[i]) for i in WEIGHTS]
    get_v[0] = load(v_hbm.at[1], v.at[0])
    get_rate = load(rate_hbm, rate)

    barrier = pltpu.get_barrier_semaphore()
    for who in ({"seq": nxt}, {"seq": prv}, {"head": side}, {"head": mirror}):
        pl.semaphore_signal(barrier, inc=1, device_id=who, device_id_type=MESH)

    get_q[0] = load(q_hbm.at[0], q.at[0])
    get_gain = load(gain_hbm, gain)
    get_ow = load(ow_hbm, ow)
    for t in range(1, ticks):
        get_k[t] = load(k_hbm.at[t + 1], k.at[t])
        get_v[t] = load(v_hbm.at[t + 1], v.at[t])
        get_q[t] = load(q_hbm.at[t], q.at[t])
    pl.semaphore_wait(barrier, 4)

    def remote(src, dst, ss, rs, who):
        return pltpu.make_async_remote_copy(
            src_ref=src, dst_ref=dst, send_sem=ss, recv_sem=rs, device_id=who, device_id_type=MESH
        )

    def wait_all_sent(buffer, sem):
        remote(buffer, buffer, sem, w_r.at[0, 0], {"seq": nxt}).wait_send()

    step = rows // LATE_PIECES
    cuts = [(i * step, (i + 1) * step) for i in reversed(range(LATE_PIECES))]
    half = LATE_PIECES // 2
    leaving = []

    def leave(src, dst):
        copy = pltpu.make_async_copy(src, dst, in_sem.at[len(leaving)])
        copy.start()
        leaving.append(copy)

    def pieces(t):
        return cuts if t == last else [(0, rows)]

    def send_near(t):
        for j, (a, b) in enumerate(pieces(t)):
            for i, hbm in enumerate((k_hbm, v_hbm)):
                piece = pl.ds(a, b - a)
                remote(
                    hbm.at[t, piece], near.at[t, i, piece], near_s, near_r.at[t + j], {"seq": nxt}
                ).start()

    def wait_near(t, a, b, j):
        both = near.at[t, :, pl.ds(a, b - a)]
        remote(both, both, near_s, near_r.at[t + j], {"seq": nxt}).wait_recv()

    def w_copy(t, i):
        return remote(w_send.at[t, i], w_recv.at[t, i], w_s, w_r.at[t, i], {"seq": nxt})

    def sv_of(t):
        column = jnp.broadcast_to(rate[t], (8, rows)).T[:, :1]
        return (column * v[t].astype(F32)).astype(BF16)

    def z_first(t, a, b, j, i):
        return remote(
            z_send.at[t, i, pl.ds(a, b - a)], z_recv.at[t, i, pl.ds(a, b - a)],
            z1_s, z1_r.at[t + j, i], {"head": first},
        )

    def z_second(t, a, b, j):
        return remote(
            z_fwd.at[t, pl.ds(a, b - a)], z_last.at[t, pl.ds(a, b - a)],
            z2_s, z2_r.at[t + j], {"head": second},
        )

    def project(combined, t, a, b, j):
        def piece(target):
            columns = pl.ds(pl.multiple_of(target * size, 128), size)
            return dot(combined, ow[:, columns]).astype(BF16)

        for i, target in enumerate((across, first)):
            z_send[t, i, a:b] = piece(target)
            z_first(t, a, b, j, i).start()
        z_keep[t, 0, a:b] = piece(second)
        z_keep[t, 1, a:b] = piece(h)

    def pass_on(t, a, b, j):
        z_first(t, a, b, j, 0).wait_recv()
        z_fwd[t, a:b] = (z_keep[t, 0, a:b].astype(F32) + z_recv[t, 0, a:b].astype(F32)).astype(BF16)
        z_second(t, a, b, j).start()

    def finish(t, a, b, j):
        z_first(t, a, b, j, 1).wait_recv()
        z_second(t, a, b, j).wait_recv()
        pair = z_keep[t, 1, a:b].astype(F32) + z_recv[t, 1, a:b].astype(F32)
        out[t, a:b] = (pair + z_last[t, a:b].astype(F32)).astype(BF16)
        piece = pl.ds(a, b - a)
        leave(out.at[t, piece], out_ref.at[t, piece])

    def waiting(copy, read):
        done = []

        def get():
            if not done:
                copy.wait()
                done.append(True)
            return read()

        return get

    def arrived(t, i):
        done = []

        def get():
            if not done:
                w_copy(t, i).wait_recv()
                done.append(True)
            return w_recv[t, i]

        return get

    own = [Rows(k.at[t], v.at[t]) for t in range(ticks)]
    prior = [Rows(near.at[t, 0], near.at[t, 1]) for t in range(ticks)]
    state = [waiting(get_w[i], lambda i=i: w[i]) for i in WEIGHTS]
    rounded = [lambda i=i: state[i]().astype(BF16) for i in WEIGHTS]
    send_near(0)

    for t in range(ticks):
        get_k[t].wait()
        get_v[t].wait()
        if t == 0:
            get_rate.wait()

        def update():
            def store(i, x):
                if t < last:
                    w_send[t, i] = x.astype(BF16)
                    w_copy(t, i).start()
                else:
                    new[i] = x
                    leave(new.at[i], new_ref.at[0, 0, i])
                    if i == 1:
                        pass_on(t, *cuts[half], half)

            fast_update(state, rounded, k[t], sv_of(t), store)
            if t < last:
                send_near(t + 1)

        def apply():
            get_q[t].wait()
            if t == 0:
                get_gain.wait()
            return normed_apply(rounded, q[t], gain[...])

        if t == 1:
            pl.when(odd == 0)(lambda: pass_on(0, 0, rows, 0))
        if t < last:
            update()
        normed = apply()
        if t == 0:
            get_ow.wait()
        scores_own = own_scores(q[t], own[t])
        if t < last:
            wait_near(t, 0, rows, 0)
            att = attend_rows(q[t], scores_own, prior[t], own[t], 0)
            project((att + normed).astype(BF16), t, 0, rows, 0)
            if t == 1:
                pl.when(odd == 1)(lambda: pass_on(0, 0, rows, 0))
            if t:
                pass_on(t, 0, rows, 0)
            rounded = [arrived(t, i) for i in WEIGHTS]
            state = [lambda f=f: f().astype(F32) for f in rounded]
        else:
            for j, (a, b) in enumerate(cuts):
                wait_near(t, a, b, j)
                att = attend_rows(q[t, a:b], scores_own[a:b], prior[t], own[t], a)
                project((att + normed[a:b]).astype(BF16), t, a, b, j)
            for j in range(half):
                pass_on(t, *cuts[j], j)
            update()
            for j in range(half + 1, LATE_PIECES):
                pass_on(t, *cuts[j], j)
            for early in range(last):
                finish(early, 0, rows, 0)
            for j, (a, b) in enumerate(cuts):
                finish(t, a, b, j)
    for copy in leaving:
        copy.wait()
    for buffer, sem in ((near, near_s), (w_send, w_s), (z_send, z1_s), (z_fwd, z2_s)):
        wait_all_sent(buffer, sem)


def write_kernel(out_ref, new_ref, out_to, new_to, sem):
    pairs = [(new_ref.at[0, 0, i], new_to.at[0, 0, i]) for i in range(new_ref.shape[2])]
    pairs += [(out_ref.at[t], out_to.at[t]) for t in range(out_ref.shape[0])]
    copies = [pltpu.make_async_copy(a, b, sem.at[i]) for i, (a, b) in enumerate(pairs)]
    for copy in copies:
        copy.start()
    for copy in copies:
        copy.wait()


def on_device(queries, key_vectors, values, learn_rates, norm_gain, out_weight, incoming):
    ticks, rows, size = queries.shape
    hbm = pl.BlockSpec(memory_space=pltpu.HBM)
    anywhere = pl.BlockSpec(memory_space=pl.ANY)
    dma = pltpu.SemaphoreType.DMA
    block = (ticks, rows, size)
    matrices = (len(WEIGHTS), size, size)
    scratch = [
        pltpu.VMEM(block, BF16),
        pltpu.VMEM(block, BF16),
        pltpu.VMEM(block, BF16),
        pltpu.VMEM((ticks, 1, rows), F32),
        pltpu.VMEM((1, size), F32),
        pltpu.VMEM(out_weight.shape, BF16),
        pltpu.VMEM(matrices, F32),
        pltpu.VMEM((ticks, 2, rows, size), BF16),
        pltpu.VMEM((ticks - 1, *matrices), BF16),
        pltpu.VMEM((ticks - 1, *matrices), BF16),
        pltpu.VMEM((ticks, 2, rows, size), BF16),
        pltpu.VMEM((ticks, 2, rows, size), BF16),
        pltpu.VMEM((ticks, 2, rows, size), BF16),
        pltpu.VMEM(block, BF16),
        pltpu.VMEM(block, BF16),
        pltpu.VMEM(block, BF16),
        pltpu.VMEM(matrices, F32),
        dma((6 + 3 * ticks,)),
        dma,
        dma((ticks - 1 + LATE_PIECES,)),
        dma,
        dma((ticks - 1, len(WEIGHTS))),
        dma,
        dma((ticks - 1 + LATE_PIECES, 2)),
        dma,
        dma((ticks - 1 + LATE_PIECES,)),
    ]
    args = (
        queries, key_vectors, values, learn_rates.transpose(0, 2, 1), norm_gain.reshape(1, size),
        out_weight, incoming,
    )
    out, outgoing = pl.pallas_call(
        layer_kernel,
        out_shape=[
            jax.ShapeDtypeStruct(queries.shape, BF16),
            jax.ShapeDtypeStruct(incoming.shape, F32),
        ],
        in_specs=[hbm] * 7,
        out_specs=[anywhere, anywhere],
        scratch_shapes=scratch,
        compiler_params=pltpu.CompilerParams(
            collective_id=0, has_side_effects=True, vmem_limit_bytes=44 << 20
        ),
        name="layer_kernel",
    )(*(pltpu.with_memory_space_constraint(x, pltpu.HBM) for x in args))
    return pl.pallas_call(
        write_kernel,
        out_shape=[jax.ShapeDtypeStruct(x.shape, x.dtype) for x in (out, outgoing)],
        in_specs=[anywhere, anywhere],
        out_specs=[anywhere, anywhere],
        scratch_shapes=[dma((ticks + len(WEIGHTS),))],
        compiler_params=pltpu.CompilerParams(vmem_limit_bytes=1 << 20),
        name="write_kernel",
    )(out, outgoing)


def solution(mesh):
    placed = (
        P(None, "seq", "head"),
        P(None, "seq", "head"),
        P(None, "seq", "head"),
        P(None, "seq", "head"),
        P("head"),
        P("head", None),
        P("seq", "head", None, None, None),
    )
    return jax.shard_map(
        on_device,
        mesh=mesh,
        in_specs=placed,
        out_specs=(P(None, "seq", "head"), P("seq", "head", None, None, None)),
        check_vma=False,
    )
```
